32 devices in a mesh: fsdp: 8 (over z, x), mat: 4 (over y, core).
Axes of the slice: x: 2, y: 2, z: 4, core: 2. Of those that a mesh axis runs over, the one named last changes fastest.
Arguments:
- grads: bfloat16 [4, 8192, 16384], P('mat', 'fsdp'), may hold values from -5000 to 5000
- p_old: bfloat16 [4, 8192, 256], P('mat', 'fsdp'), may hold values from -2 to 2
- p_new: bfloat16 [4, 8192, 256], P('mat', 'fsdp'), may hold values from -2 to 2
- m_old: float32 [4, 16384, 256], P('mat', 'fsdp'), may hold values from -4 to 4
- v_old: float32 [4, 16384, 256], P('mat', 'fsdp'), may hold values from 0.003 to 0.03
Outputs:
- update: bfloat16 [4, 8192, 16384], P('mat', 'fsdp')
- m_new: float32 [4, 16384, 256], P('mat', 'fsdp')
- v_new: float32 [4, 16384, 256], P('mat', 'fsdp')
The draws below stay inside these ranges and needn't reach their ends.
All inputs are finite; a program needn't handle non-finite values.
Results may differ from the reference program's by a relative error of at most 0.0046.
Values may be sent and summed in bfloat16 or wider, within the bound.
A program may use at most 320 MiB of HBM per device.

```python
import math
import jax
import jax.numpy as jnp
from jax import lax

D = 8192
COLS = 16384
RANK = 256
NMAT = 4


def basis_pair(key):
    base = jnp.clip(jax.random.normal(jax.random.fold_in(key, 11), (NMAT, D, RANK), jnp.float32), -6.0, 6.0)
    other = jnp.clip(jax.random.normal(jax.random.fold_in(key, 12), (NMAT, D, RANK), jnp.float32), -6.0, 6.0)
    base = base / jnp.sqrt(jnp.float32(D))
    other = other / jnp.sqrt(jnp.float32(D))
    fresh = 0.6 * base + 0.45 * jnp.roll(base, 1, axis=2) + 0.3 * jnp.roll(base, 5, axis=2) + 0.55 * other
    return (base, fresh)


def draw_p_old(key, part):
    return basis_pair(key)[0].astype(jnp.bfloat16)


def draw_p_new(key, part):
    return basis_pair(key)[1].astype(jnp.bfloat16)


def draw_grads(key, part):
    key_a = jax.random.fold_in(key, 21)
    key_b = jax.random.fold_in(key, 22)
    key_c = jax.random.fold_in(key, 23)
    position = jnp.arange(D, dtype=jnp.float32) / D
    matrix_pos = jnp.arange(NMAT, dtype=jnp.float32) / max(NMAT - 1, 1)
    noise = jnp.clip(jax.random.normal(key_a, (NMAT, D, COLS), jnp.float32), -6.0, 6.0)
    trend = 0.24
    row_log = jax.random.uniform(key_b, (NMAT, D, 1), jnp.float32) + trend * position[None, :, None]
    col_log = jax.random.uniform(key_c, (NMAT, 1, COLS), jnp.float32)
    scale = jnp.power(10.0, row_log + col_log) * jnp.power(3.0, 0.5 * matrix_pos)[:, None, None]
    return (noise * scale).astype(jnp.bfloat16)


def level_of(stream_key, shape, split, smallest, high):
    level = 1.0
    for axis_at, shards_of in split:
        heights = jax.random.uniform(jax.random.fold_in(jax.random.fold_in(stream_key, 6), axis_at), (shards_of,), jnp.float32, smallest / len(split), high / len(split))
        level = level * jnp.repeat(jnp.exp(heights), shape[axis_at] // shards_of).reshape((-1,) + (1,) * (len(shape) - 1 - axis_at))
    return level


def gaussian(own_key, shape, spread, reach, pieces=(), kind=jnp.bfloat16):
    values = jax.random.normal(own_key, shape, jnp.float32) * spread
    if len(pieces) > 0:
        values = level_of(own_key, shape, pieces, -0.22, 0.18) * values
    return jnp.clip(values, min=-reach, max=reach).astype(kind)


def setup_inputs(seed: int = 0) -> dict:
    splits = jax.random.split(jax.random.key(seed), 6)
    grads = draw_grads(jax.random.fold_in(splits[5], 71), 0)
    p_old = draw_p_old(jax.random.fold_in(splits[5], 71), 0)
    p_new = draw_p_new(jax.random.fold_in(splits[5], 71), 0)
    m_old = gaussian(splits[3], (NMAT, COLS, RANK), 0.3, 4.0, ((0, 4), (1, 8)), jnp.float32)
    v_old = jnp.clip(jnp.exp(math.log(0.03) - 2.3025851 * jax.random.uniform(splits[4], (NMAT, COLS, RANK), jnp.float32) ** level_of(splits[4], (NMAT, COLS, RANK), ((0, 4), (1, 8)), -0.2, 0.2)), 0.003, 0.03)
    return dict(grads=grads, p_old=p_old, p_new=p_new, m_old=m_old, v_old=v_old)


def reference(grads, p_old, p_new, m_old, v_old):
    total = jnp.sum(jnp.square(grads.astype(jnp.float32)))
    clip = jnp.minimum(1.0, 0.5 / jnp.sqrt(total / (NMAT * D * COLS) + 1e-06))
    updates = []
    firsts = []
    seconds = []
    for index in range(NMAT):
        gram = jnp.dot(p_new[index].T, p_old[index], preferred_element_type=jnp.float32)
        rot_m = jnp.dot(m_old[index], gram.T, precision=lax.Precision.HIGHEST)
        rot_v = jnp.dot(v_old[index], (gram * gram).T, precision=lax.Precision.HIGHEST)
        proj = clip * jnp.dot(grads[index].T, p_new[index], preferred_element_type=jnp.float32)
        first = 0.9 * rot_m + 0.1 * proj
        second = 0.99 * rot_v + 0.01 * proj * proj
        dirn = (first / (jnp.sqrt(second) + 1e-08)).astype(jnp.bfloat16)
        upd = jnp.dot(p_new[index], dirn.T, preferred_element_type=jnp.float32).astype(jnp.bfloat16)
        updates.append(upd)
        firsts.append(first)
        seconds.append(second)
    return (jnp.stack(updates), jnp.stack(firsts), jnp.stack(seconds))
```

```python
import functools

import jax
import jax.numpy as jnp
from jax import lax
from jax.experimental import pallas as pl
from jax.experimental.pallas import tpu as pltpu
from jax.sharding import PartitionSpec as P

CHUNKS = 4


def plain(mat_count, fsdp_count, grads, p_old, p_new, m_old, v_old):
    grad, basis_old, basis_new = grads[0], p_old[0], p_new[0]
    size = mat_count * fsdp_count * grad.shape[0] * grad.shape[1]
    total = lax.psum(jnp.sum(jnp.square(grad.astype(jnp.float32))), ("fsdp", "mat"))
    clip = jnp.minimum(1.0, 0.5 / jnp.sqrt(total / size + 1e-06))
    gram = lax.psum(
        lax.dot_general(basis_new, basis_old, (((0,), (0,)), ((), ())), preferred_element_type=jnp.float32),
        "fsdp",
    )
    rot_m = jnp.dot(m_old[0], gram.T, precision=lax.Precision.HIGHEST)
    rot_v = jnp.dot(v_old[0], (gram * gram).T, precision=lax.Precision.HIGHEST)
    proj = clip * lax.psum_scatter(
        lax.dot_general(grad, basis_new, (((0,), (0,)), ((), ())), preferred_element_type=jnp.float32),
        "fsdp",
        scatter_dimension=0,
        tiled=True,
    )
    first = 0.9 * rot_m + 0.1 * proj
    second = 0.99 * rot_v + 0.01 * proj * proj
    dirn = (first / (jnp.sqrt(second) + 1e-08)).astype(jnp.bfloat16)
    upd = lax.dot_general(
        basis_new,
        lax.all_gather(dirn, "fsdp", axis=0, tiled=True),
        (((1,), (1,)), ((), ())),
        preferred_element_type=jnp.float32,
    ).astype(jnp.bfloat16)
    return (upd[None], first[None], second[None])


def project(grad_ref, basis_ref, square_ref):
    block = grad_ref[...]
    wide = block.astype(jnp.float32)
    rows, cols = wide.shape
    part = jnp.sum((wide * wide).reshape(rows // 8, 8, cols), axis=0)

    @pl.when(pl.program_id(0) == 0)
    def _():
        square_ref[...] = part

    @pl.when(pl.program_id(0) > 0)
    def _():
        square_ref[...] += part

    return lax.dot_general(
        block, basis_ref[...], (((0,), (0,)), ((), ())), preferred_element_type=jnp.float32
    )


def far_kernel(at_ref, grad_ref, basis_ref, *rest):
    out_ref, square_ref = rest[-2:]
    out_ref[0] = project(grad_ref, basis_ref, square_ref).astype(jnp.bfloat16)


def near_kernel(at_ref, grad_ref, basis_ref, out_ref, square_ref):
    out_ref[0] = project(grad_ref, basis_ref, square_ref)


def relay_kernel(value_ref, gate_ref, out_ref):
    out_ref[...] = value_ref[...]


def normalize_kernel(count, *refs):
    own_ref, part_refs, (m_ref, v_ref, clip_ref) = refs[0], refs[1:count], refs[count : count + 3]
    first_ref, second_ref, dirn_ref = refs[-3:]
    proj = own_ref[...]
    for part_ref in part_refs:
        proj = proj + part_ref[...].astype(jnp.float32)
    proj = clip_ref[0, 0] * proj
    first = 0.9 * m_ref[...] + 0.1 * proj
    second = 0.99 * v_ref[...] + 0.01 * proj * proj
    first_ref[...] = first
    second_ref[...] = second
    dirn_ref[...] = (first / (jnp.sqrt(second) + 1e-08)).astype(jnp.bfloat16)


def update_kernel(at_ref, basis_ref, dirn_ref, *rest):
    out_ref, token_ref = rest[-2:]
    out_ref[...] = lax.dot_general(
        basis_ref[...], dirn_ref[0], (((1,), (1,)), ((), ())), preferred_element_type=jnp.float32
    ).astype(jnp.bfloat16)
    token_ref[...] = jnp.zeros_like(token_ref)


def chunked(mat_count, fsdp_count, grads, p_old, p_new, m_old, v_old):
    grad, basis_old, basis_new, first_old, second_old = grads[0], p_old[0], p_new[0], m_old[0], v_old[0]
    rows, columns = grad.shape
    rank = basis_new.shape[1]
    line = fsdp_count // 2
    size = mat_count * fsdp_count * rows * columns
    width = columns // fsdp_count // CHUNKS
    me = lax.axis_index("fsdp")
    z, x = me // 2, me % 2

    def swap(value, away, axis="fsdp", count=fsdp_count):
        return lax.ppermute(value, axis, [(i, i ^ away) for i in range(count)])

    def places(side, chunk):
        return jnp.stack([((z ^ d) * 2 + (x ^ side)) * CHUNKS + chunk for d in range(line)]).astype(jnp.int32)

    deep = pl.BlockSpec((1, width, rank), lambda i, at: (i, 0, 0))
    whole_basis = pl.BlockSpec((rows, rank), lambda i, at: (0, 0))
    tall = pl.BlockSpec((rows, width), lambda i, at: (0, at[i]))
    held_spec = pl.BlockSpec(memory_space=pl.ANY)
    squares = pl.BlockSpec((8, width), lambda i, at: (0, 0))
    cost = pl.CostEstimate(
        flops=2 * line * rows * width * rank, bytes_accessed=2 * line * rows * width, transcendentals=0
    )
    params = pltpu.CompilerParams(dimension_semantics=("arbitrary",))

    def partial(side, chunk, kind, *gate):
        return pl.pallas_call(
            near_kernel if side == 0 else far_kernel,
            out_shape=(
                jax.ShapeDtypeStruct((line, width, rank), kind),
                jax.ShapeDtypeStruct((8, width), jnp.float32),
            ),
            grid_spec=pltpu.PrefetchScalarGridSpec(
                num_scalar_prefetch=1, grid=(line,), in_specs=[tall, whole_basis] + [held_spec] * len(gate),
                out_specs=(deep, squares),
            ),
            compiler_params=params,
            cost_estimate=cost,
            name="near" if side == 0 else "far",
        )(places(side, chunk), grad, basis_new, *gate)

    def update(side, chunk, dirns, out):
        held = () if out is None else (out,)
        return pl.pallas_call(
            update_kernel,
            out_shape=(
                jax.ShapeDtypeStruct((rows, columns), jnp.bfloat16),
                jax.ShapeDtypeStruct((8, 128), jnp.float32),
            ),
            grid_spec=pltpu.PrefetchScalarGridSpec(
                num_scalar_prefetch=1,
                grid=(line,),
                in_specs=[whole_basis, deep] + [pl.BlockSpec(memory_space=pl.ANY)] * len(held),
                out_specs=(tall, pl.BlockSpec((8, 128), lambda i, at: (0, 0))),
            ),
            input_output_aliases={} if out is None else {3: 0},
            compiler_params=params,
            cost_estimate=cost,
            name="update",
        )(places(side, chunk), basis_new, dirns, *held)

    def after(value, gate):
        vmem = pl.BlockSpec(memory_space=pltpu.VMEM)
        return pl.pallas_call(
            relay_kernel,
            out_shape=jax.ShapeDtypeStruct(value.shape, value.dtype),
            in_specs=[vmem, held_spec],
            out_specs=vmem,
            name="relay",
        )(value, gate)

    gram = lax.dot_general(
        basis_new, basis_old, (((0,), (0,)), ((), ())), preferred_element_type=jnp.float32
    )
    own_gram = gram
    gram = gram + swap(gram, 1)
    away = 2
    while away < fsdp_count:
        gram = gram + swap(gram, away)
        away *= 2

    fars = [partial(1, k, jnp.bfloat16, *([own_gram, gram][k : k + 1])) for k in range(CHUNKS)]
    nears = [partial(0, k, jnp.float32) for k in range(CHUNKS)]
    total = jnp.full((8, 128), sum(jnp.sum(part[1]) for part in fars + nears), jnp.float32)
    total = total + swap(total, 1)
    came = [swap(fars[k][0] if k < 2 else after(fars[k][0], total), 1) for k in range(CHUNKS)]
    away = 2
    while away < fsdp_count:
        total = total + swap(total, away)
        away *= 2
    away = 1
    while away < mat_count:
        total = total + swap(total, away, "mat", mat_count)
        away *= 2
    clip = jnp.minimum(1.0, 0.5 / jnp.sqrt(total[0, 0] / size + 1e-06))
    rot_m = jnp.dot(first_old, gram.T, precision=lax.Precision.HIGHEST)
    rot_v = jnp.dot(second_old, (gram * gram).T, precision=lax.Precision.HIGHEST)

    owns, arrived = [], []
    for k in range(CHUNKS):
        both = [nears[k][0][d] + came[k][d].astype(jnp.float32) for d in range(line)]
        owns.append(both[0])
        arrived.append([swap(both[d].astype(jnp.bfloat16), 2 * d) for d in range(1, line)])

    firsts, seconds, stacks, others = [], [], {}, {}
    state = {"out": None, "token": None}

    def normalize(k):
        gate = () if state["token"] is None else (state["token"],)
        flat = pl.BlockSpec((width, rank), lambda i: (0, 0))
        piece = pl.BlockSpec((width, rank), lambda i: (k, 0))
        wide = jax.ShapeDtypeStruct((width, rank), jnp.float32)
        first, second, dirn = pl.pallas_call(
            functools.partial(normalize_kernel, line),
            grid=(1,),
            out_shape=(wide, wide, jax.ShapeDtypeStruct((width, rank), jnp.bfloat16)),
            in_specs=[flat] * line
            + [piece, piece, pl.BlockSpec(memory_space=pltpu.SMEM)]
            + [held_spec] * len(gate),
            out_specs=(flat,) * 3,
            cost_estimate=pl.CostEstimate(
                flops=20 * width * rank, bytes_accessed=32 * width * rank, transcendentals=width * rank
            ),
            name="normalize",
        )(owns[k], *arrived[k], rot_m, rot_v, clip.reshape(1, 1), *gate)
        firsts.append(first)
        seconds.append(second)
        stacks[k] = jnp.stack([dirn] + [swap(dirn, 2 * d) for d in range(1, line)])

    def exchange(k):
        others[k] = swap(stacks[k] if state["token"] is None else after(stacks[k], state["token"]), 1)

    def write(side, k):
        state["out"], state["token"] = update(side, k, others[k] if side else stacks[k], state["out"])

    normalize(0)
    normalize(1)
    exchange(0)
    exchange(1)
    for k in range(CHUNKS):
        if k + 2 < CHUNKS:
            if k == 0:
                write(0, 0)
                normalize(2)
                write(0, 1)
            write(1, k)
            if k == 0:
                normalize(3)
            else:
                exchange(2)
                write(0, 2)
                exchange(3)
        else:
            write(1, k)
            if k + 1 < CHUNKS:
                write(0, k + 1)
    return (state["out"][None], jnp.concatenate(firsts)[None], jnp.concatenate(seconds)[None])


def solution(mesh):
    fsdp_count, mat_count = mesh.shape["fsdp"], mesh.shape["mat"]
    placed = P("mat", "fsdp", None)
    body = chunked if fsdp_count <= 16 else plain
    return jax.shard_map(
        functools.partial(body, mat_count, fsdp_count),
        mesh=mesh,
        in_specs=(placed,) * 5,
        out_specs=(placed,) * 3,
        check_vma=False,
    )
```
